32 devices in a mesh: groups: 2 (over y), region: 16 (over z, x, core).
Axes of the slice: x: 2, y: 2, z: 4, core: 2. Of those that a mesh axis runs over, the one named last changes fastest.
Arguments:
- noisy_future: bfloat16 [8192, 2, 512], P(('groups', 'region')), parts along dimension 0, may hold values from -6 to 6
- history: bfloat16 [8192, 16, 512], P(('groups', 'region')), parts along dimension 0, may hold values from -6 to 6
- norm_gain: float32 [512], replicated, may hold values from 0.1 to 1.9
- w_query: bfloat16 [512, 512], replicated, may hold values from -0.25 to 0.25
- w_key: bfloat16 [512, 512], replicated, may hold values from -0.25 to 0.25
- w_value: bfloat16 [512, 512], replicated, may hold values from -0.25 to 0.25
- w_out: bfloat16 [512, 512], replicated, may hold values from -1.5 to 1.5
- nbr_owner: int32 [64, 4], P(('groups', 'region')), parts along dimension 0, may hold values from 0 to 15, as said below
- nbr_tile: int32 [64, 4], P(('groups', 'region')), parts along dimension 0, may hold values from 0 to 1
- nbr_count: int32 [64], P(('groups', 'region')), parts along dimension 0, may hold values from 1 to 4, as said below
- dest_shard: int32 [8192], P(('groups', 'region')), parts along dimension 0, may hold values from 0 to 15, as said below
- dest_slot: int32 [8192], P(('groups', 'region')), parts along dimension 0, may hold values from 0 to 255
Outputs:
- next_cache: bfloat16 [8192, 16, 512], P(('groups', 'region')), parts along dimension 0
The draws below stay inside these ranges and needn't reach their ends.
There are 2 independent parts, one for each index of `groups`. The reference program is written for one: setup_inputs(seed, part) draws one part's arguments, and reference() takes and returns one part's arrays. A program takes and returns all parts, laid end to end along the dimension named above; an argument that names none is the same for every part. Nothing has to cross between parts.
Inputs may be any that keep to these rules, and one draw needn't show every extreme that they name: `nbr_owner`: entry j of row t names the owner of neighbour tile j of agent tile t; it lies within 2 shards of t // 2. Only the first nbr_count[t] entries of row t are neighbours; the others are ignored. `dest_shard`: with dest_slot, every agent goes to a distinct (shard, slot) pair, so each shard receives exactly 256 agents. From one shard at most 32 agents go to one destination shard, and in every draw some shard sends exactly 32 to some destination.
All inputs are finite; a program needn't handle non-finite values.
Results may differ from the reference program's by a relative error of at most 0.003.
Values may be sent and summed in bfloat16 or wider, within the bound.
A program may use at most 128 MiB of HBM per device.

```python
import jax
import jax.numpy as jnp
from jax import lax

D = 512
HEADS = 8
HEAD = 64
HIST = 16
FUTURE = 2
TILE = 128
NBR = 4
R_NB = 2
TILES_DEV = 2
AGENTS_DEV = 256
AGENTS = 4096
N_REGION = 16


def draw_nbr_owner(key, part):
    tile_total = AGENTS // TILE
    home = jnp.arange(tile_total, dtype=jnp.int32) // TILES_DEV
    offsets = jax.random.randint(jax.random.fold_in(key, 11), (tile_total, NBR), -R_NB, R_NB + 1, dtype=jnp.int32)
    offsets = offsets.at[0, 0].set(-R_NB).at[tile_total - 1, 0].set(R_NB)
    return jnp.clip(home[:, None] + offsets, 0, N_REGION - 1).astype(jnp.int32)


def draw_nbr_tile(key, part):
    tile_total = AGENTS // TILE
    picks = jax.random.randint(jax.random.fold_in(key, 12), (tile_total, NBR), 0, TILES_DEV, dtype=jnp.int32)
    return picks.at[0, 0].set(TILES_DEV - 1).at[0, 1].set(0)


def draw_nbr_count(key, part):
    tile_total = AGENTS // TILE
    counts = jax.random.randint(jax.random.fold_in(key, 13), (tile_total,), 1, NBR + 1, dtype=jnp.int32)
    return counts.at[0].set(NBR).at[1].set(1)


def migration_plan(key):
    base = jax.random.fold_in(key, 21)
    key_shift, key_rows, key_slots = jax.random.split(base, 3)
    blocks = N_REGION // 2
    capacity = 2 * AGENTS_DEV // N_REGION
    shifts = jax.random.permutation(key_shift, N_REGION)[:blocks].astype(jnp.int32)
    row_order = jax.vmap(lambda one_key: jax.random.permutation(one_key, AGENTS_DEV))(jax.random.split(key_rows, N_REGION)).astype(jnp.int32)
    inner = jax.vmap(lambda one_key: jax.random.permutation(one_key, capacity))(jax.random.split(key_slots, N_REGION * blocks)).astype(jnp.int32)
    inner = inner.reshape(N_REGION, AGENTS_DEV)
    position = jnp.arange(AGENTS_DEV, dtype=jnp.int32)
    block_of = position // capacity
    source = jnp.arange(N_REGION, dtype=jnp.int32)[:, None]
    target_shard = (source + shifts[block_of][None, :]) % N_REGION
    target_slot = block_of[None, :] * capacity + inner
    global_rows = (source * AGENTS_DEV + row_order).reshape(-1)
    dest = jnp.zeros((AGENTS,), jnp.int32).at[global_rows].set(target_shard.reshape(-1).astype(jnp.int32))
    slot = jnp.zeros((AGENTS,), jnp.int32).at[global_rows].set(target_slot.reshape(-1).astype(jnp.int32))
    return (dest, slot)


def draw_dest_shard(key, part):
    return migration_plan(key)[0]


def draw_dest_slot(key, part):
    return migration_plan(key)[1]


def block_levels(stream_key, shape, cuts, low, largest):
    def one(dim, blocks):
        draws = jax.random.uniform(jax.random.fold_in(jax.random.fold_in(stream_key, 6), dim), (blocks,), jnp.float32, low / len(cuts), largest / len(cuts))
        return jnp.repeat(jnp.exp(draws), shape[dim] // blocks).reshape((-1,) + (1,) * (len(shape) - dim - 1))

    gain = one(*cuts[0])
    for cut in cuts[1:]:
        gain = gain * one(*cut)
    return gain


def centred(own_key, extent, spread, reach, cuts=(), kind=jnp.bfloat16):
    values = jax.random.normal(own_key, extent, jnp.float32) * spread
    if len(cuts) > 0:
        values = block_levels(own_key, extent, cuts, -0.22, 0.18) * values
    return jnp.clip(values, min=-reach, max=reach).astype(kind)


def setup_inputs(seed: int = 0, part: int = 0) -> dict:
    keys = jax.random.split(jax.random.key(seed), 13)
    part_keys = jax.random.split(jax.random.fold_in(keys[12], part), 13)
    noisy_future = centred(part_keys[0], (AGENTS, FUTURE, D), 1.0, 6.0, ((0, 16),))
    history = centred(part_keys[1], (AGENTS, HIST, D), 1.0, 6.0, ((0, 16),))
    norm_gain = jnp.clip(1.0 + 0.18 * jax.random.normal(keys[2], (D,), jnp.float32), 0.1, 1.9)
    w_query = centred(keys[3], (D, D), D ** -0.5, 0.25)
    w_key = centred(keys[4], (D, D), D ** -0.5, 0.25)
    w_value = centred(keys[5], (D, D), D ** -0.5, 0.25)
    w_out = centred(keys[6], (D, D), 0.25, 1.5)
    nbr_owner = draw_nbr_owner(jax.random.fold_in(jax.random.fold_in(keys[12], part), 71), part)
    nbr_tile = draw_nbr_tile(jax.random.fold_in(jax.random.fold_in(keys[12], part), 71), part)
    nbr_count = draw_nbr_count(jax.random.fold_in(jax.random.fold_in(keys[12], part), 71), part)
    dest_shard = draw_dest_shard(jax.random.fold_in(jax.random.fold_in(keys[12], part), 71), part)
    dest_slot = draw_dest_slot(jax.random.fold_in(jax.random.fold_in(keys[12], part), 71), part)
    return {"noisy_future": noisy_future, "history": history, "norm_gain": norm_gain, "w_query": w_query, "w_key": w_key, "w_value": w_value, "w_out": w_out, "nbr_owner": nbr_owner, "nbr_tile": nbr_tile, "nbr_count": nbr_count, "dest_shard": dest_shard, "dest_slot": dest_slot}


def normed_rows(states, norm_gain):
    values = states.astype(jnp.float32)
    inverse = lax.rsqrt(lax.optimization_barrier(jnp.mean(values * values, axis=-1, keepdims=True)) + 1e-05)
    return (values * inverse * norm_gain).astype(jnp.bfloat16)

def head_normed(projected, head_count):
    split_heads = projected.reshape(projected.shape[0], head_count, -1)
    inverse = lax.rsqrt(lax.optimization_barrier(jnp.mean(split_heads * split_heads, axis=-1, keepdims=True)) + 1e-06)
    return (split_heads * inverse).astype(jnp.bfloat16)

def neighbour_part(queries_tile, keys_tile, values_tile, key_valid, local_sum, score_scale):
    scores = jnp.einsum('qnd,knd->nqk', queries_tile.astype(jnp.float32), keys_tile.astype(jnp.float32)) * score_scale
    weights = jnp.exp(scores) * key_valid[None, None, :]
    denominator = local_sum + lax.optimization_barrier(jnp.sum(weights, axis=-1))
    probs = (weights / denominator[..., None]).astype(jnp.bfloat16)
    mixed_part = jnp.einsum('nqk,knd->qnd', probs.astype(jnp.float32), values_tile.astype(jnp.float32))
    return (mixed_part, denominator)

def reference(noisy_future, history, norm_gain, w_query, w_key, w_value, w_out, nbr_owner, nbr_tile, nbr_count, dest_shard, dest_slot):
    score_scale = 1.0 / HEAD ** 0.5
    last_normed = normed_rows(history[:, HIST - 1], norm_gain)
    keys_last = head_normed(jnp.dot(last_normed, w_key, preferred_element_type=jnp.float32), HEADS)
    values_last = jnp.dot(last_normed, w_value, preferred_element_type=jnp.float32).astype(jnp.bfloat16)
    keys_last = keys_last.reshape(AGENTS // TILE, TILE, D)
    values_last = values_last.reshape(AGENTS // TILE, TILE, D)

    def shard_step(inputs):
        future_rows, hist_rows, owner_rows, tile_ids, count_rows = inputs
        tile_count = owner_rows.shape[0]
        future_normed = normed_rows(future_rows.reshape(-1, D), norm_gain)
        queries = head_normed(jnp.dot(future_normed, w_query, preferred_element_type=jnp.float32), HEADS)
        keys_new = head_normed(jnp.dot(future_normed, w_key, preferred_element_type=jnp.float32), HEADS)
        values_new = jnp.dot(future_normed, w_value, preferred_element_type=jnp.float32).astype(jnp.bfloat16)
        hist_normed = normed_rows(hist_rows.reshape(-1, D), norm_gain)
        keys_hist = head_normed(jnp.dot(hist_normed, w_key, preferred_element_type=jnp.float32), HEADS)
        values_hist = jnp.dot(hist_normed, w_value, preferred_element_type=jnp.float32).astype(jnp.bfloat16)
        keys_local = jnp.concatenate([keys_hist.reshape(AGENTS_DEV, HIST, HEADS, HEAD), keys_new.reshape(AGENTS_DEV, FUTURE, HEADS, HEAD)], axis=1)
        values_local = jnp.concatenate([values_hist.reshape(AGENTS_DEV, HIST, HEADS, HEAD), values_new.reshape(AGENTS_DEV, FUTURE, HEADS, HEAD)], axis=1)
        query_four = queries.reshape(AGENTS_DEV, FUTURE, HEADS, HEAD)
        local_scores = jnp.einsum('acnd,aknd->anck', query_four.astype(jnp.float32), keys_local.astype(jnp.float32)) * score_scale
        local_weights = jnp.exp(local_scores)
        local_sum = lax.optimization_barrier(jnp.sum(local_weights, axis=-1))
        local_sum_tiles = local_sum.reshape(tile_count, TILE, HEADS, FUTURE).transpose(0, 2, 1, 3).reshape(tile_count, HEADS, TILE * FUTURE)
        tile_index = (owner_rows * TILES_DEV + tile_ids).astype(jnp.int32)
        keys_nbr = keys_last[tile_index].reshape(tile_count, NBR * TILE, HEADS, HEAD)
        values_nbr = values_last[tile_index].reshape(tile_count, NBR * TILE, HEADS, HEAD)
        key_valid = (jnp.arange(NBR, dtype=jnp.int32)[None, :] < count_rows[:, None]).astype(jnp.float32)
        key_valid = jnp.repeat(key_valid, TILE, axis=1)
        query_tiles = queries.reshape(tile_count, TILE * FUTURE, HEADS, HEAD)
        mixed_nbr, denominator = lax.map(lambda parts: neighbour_part(*parts, score_scale), (query_tiles, keys_nbr, values_nbr, key_valid, local_sum_tiles))
        denominator_local = denominator.reshape(tile_count, HEADS, TILE, FUTURE).transpose(0, 2, 1, 3).reshape(AGENTS_DEV, HEADS, FUTURE)
        local_probs = (local_weights / denominator_local[..., None]).astype(jnp.bfloat16)
        mixed_local = jnp.einsum('anck,aknd->acnd', local_probs.astype(jnp.float32), values_local.astype(jnp.float32))
        mixed = (mixed_local.reshape(-1, HEADS, HEAD) + mixed_nbr.reshape(-1, HEADS, HEAD)).astype(jnp.bfloat16).reshape(-1, D)
        update = jnp.dot(mixed, w_out, preferred_element_type=jnp.float32)
        denoised = (future_rows.reshape(-1, D).astype(jnp.float32) + update).astype(jnp.bfloat16).reshape(AGENTS_DEV, FUTURE, D)
        return jnp.concatenate([hist_rows[:, FUTURE:], denoised], axis=1)
    new_cache = lax.map(shard_step, (noisy_future.reshape(N_REGION, AGENTS_DEV, FUTURE, D), history.reshape(N_REGION, AGENTS_DEV, HIST, D), nbr_owner.reshape(N_REGION, TILES_DEV, NBR), nbr_tile.reshape(N_REGION, TILES_DEV, NBR), nbr_count.reshape(N_REGION, TILES_DEV)))
    new_cache = new_cache.reshape(AGENTS, HIST, D)
    target = (dest_shard * AGENTS_DEV + dest_slot).astype(jnp.int32)
    return jnp.zeros((AGENTS, HIST, D), jnp.bfloat16).at[target].set(new_cache)
```

```python
import jax
import jax.numpy as jnp
from jax import lax
from jax.sharding import PartitionSpec as P

HEADS = 8
NBR = 4
R_NB = 2


def shifted(value, axis, steps):
    count = lax.axis_size(axis)
    initial, last = (max(0, -steps), min(count, count - steps))
    return lax.ppermute(value, axis, [(source, source + steps) for source in range(initial, last)])


def normed_rows(states, norm_gain):
    values = states.astype(jnp.float32)
    inverse = lax.rsqrt(jnp.mean(values * values, axis=-1, keepdims=True) + 1e-05)
    return (values * inverse * norm_gain).astype(jnp.bfloat16)


def head_normed(projected, head_count):
    split_heads = projected.reshape(projected.shape[0], head_count, -1)
    inverse = lax.rsqrt(jnp.mean(split_heads * split_heads, axis=-1, keepdims=True) + 1e-06)
    return (split_heads * inverse).astype(jnp.bfloat16)


def neighbour_part(queries_tile, keys_tile, values_tile, key_valid, local_sum, score_scale):
    scores = (
        jnp.einsum("qnd,knd->nqk", queries_tile, keys_tile, preferred_element_type=jnp.float32)
        * score_scale
    )
    weights = jnp.exp(scores) * key_valid[None, None, :]
    denominator = local_sum + jnp.sum(weights, axis=-1)
    probs = (weights / denominator[..., None]).astype(jnp.bfloat16)
    mixed_part = jnp.einsum("nqk,knd->qnd", probs, values_tile, preferred_element_type=jnp.float32)
    return (mixed_part, denominator)


def per_device(
    noisy_future,
    history,
    norm_gain,
    w_query,
    w_key,
    w_value,
    w_out,
    nbr_owner,
    nbr_tile,
    nbr_count,
    dest_shard,
    dest_slot,
):
    agent_count, future_len, model_width = noisy_future.shape
    hist_len = history.shape[1]
    tile_count = nbr_owner.shape[0]
    tile_rows = agent_count // tile_count
    head_size = model_width // HEADS
    score_scale = 1.0 / head_size**0.5
    regions = lax.axis_size("region")
    my_index = lax.axis_index("region")
    capacity = 2 * agent_count // regions
    one_hot = (dest_shard[:, None] == jnp.arange(regions, dtype=jnp.int32)[None, :]).astype(
        jnp.float32
    )
    before = jnp.tril(jnp.ones((agent_count, agent_count), jnp.bfloat16), -1)
    earlier = jnp.dot(before, one_hot.astype(jnp.bfloat16), preferred_element_type=jnp.float32)
    row_rank = jnp.sum(earlier * one_hot, axis=1).astype(jnp.int32)
    buffer_pos = dest_shard * capacity + row_rank
    packer = jnp.arange(regions * capacity, dtype=jnp.int32)[:, None] == buffer_pos[None, :]
    slot_ids = jnp.max(jnp.where(packer, dest_slot[None, :], -1), axis=1)
    packer = packer.astype(jnp.bfloat16)

    def exchange(rows):
        return lax.all_to_all(rows, "region", split_axis=0, concat_axis=0, tiled=True)

    last_normed = normed_rows(history[:, hist_len - 1], norm_gain)
    window_states = []
    for offset in range(-R_NB, R_NB + 1):
        if offset == 0:
            arrived = last_normed
        else:
            arrived = shifted(last_normed, "region", -offset)
        window_states.append(arrived)
    kept = history.reshape(agent_count, hist_len * model_width)[:, future_len * model_width :]
    packed = jnp.dot(packer, kept, preferred_element_type=jnp.float32).astype(jnp.bfloat16)
    slot_lanes = jnp.broadcast_to(slot_ids[:, None], (regions * capacity, 128))
    moved_kept = exchange(jnp.concatenate([packed, slot_lanes.astype(jnp.bfloat16)], axis=1))
    future_normed = normed_rows(noisy_future.reshape(-1, model_width), norm_gain)
    queries = head_normed(
        jnp.dot(future_normed, w_query, preferred_element_type=jnp.float32), HEADS
    )
    keys_new = head_normed(jnp.dot(future_normed, w_key, preferred_element_type=jnp.float32), HEADS)
    values_new = jnp.dot(future_normed, w_value, preferred_element_type=jnp.float32).astype(
        jnp.bfloat16
    )
    hist_normed = normed_rows(history.reshape(-1, model_width), norm_gain)
    keys_hist = head_normed(jnp.dot(hist_normed, w_key, preferred_element_type=jnp.float32), HEADS)
    values_hist = jnp.dot(hist_normed, w_value, preferred_element_type=jnp.float32).astype(
        jnp.bfloat16
    )
    tile_index = (nbr_owner - my_index + R_NB) * tile_count + nbr_tile
    stacked_states = jnp.stack(window_states).reshape(-1, tile_rows, model_width)
    picked = jnp.take(stacked_states, tile_index, axis=0).reshape(-1, model_width)
    keys_nbr = head_normed(jnp.dot(picked, w_key, preferred_element_type=jnp.float32), HEADS)
    keys_nbr = keys_nbr.reshape(tile_count, NBR * tile_rows, HEADS, head_size)
    values_nbr = jnp.dot(picked, w_value, preferred_element_type=jnp.float32).astype(jnp.bfloat16)
    values_nbr = values_nbr.reshape(tile_count, NBR * tile_rows, HEADS, head_size)
    keys_local = jnp.concatenate(
        [
            keys_hist.reshape(agent_count, hist_len, HEADS, head_size),
            keys_new.reshape(agent_count, future_len, HEADS, head_size),
        ],
        axis=1,
    )
    values_local = jnp.concatenate(
        [
            values_hist.reshape(agent_count, hist_len, HEADS, head_size),
            values_new.reshape(agent_count, future_len, HEADS, head_size),
        ],
        axis=1,
    )
    query_four = queries.reshape(agent_count, future_len, HEADS, head_size)
    local_scores = (
        jnp.einsum("acnd,aknd->anck", query_four, keys_local, preferred_element_type=jnp.float32)
        * score_scale
    )
    local_weights = jnp.exp(local_scores)
    local_sum = jnp.sum(local_weights, axis=-1)
    local_sum_tiles = (
        local_sum.reshape(tile_count, tile_rows, HEADS, future_len)
        .transpose(0, 2, 1, 3)
        .reshape(tile_count, HEADS, tile_rows * future_len)
    )
    key_valid = (jnp.arange(NBR, dtype=jnp.int32)[None, :] < nbr_count[:, None]).astype(jnp.float32)
    key_valid = jnp.repeat(key_valid, tile_rows, axis=1)
    query_tiles = queries.reshape(tile_count, tile_rows * future_len, HEADS, head_size)
    mixed_nbr, denominator = lax.map(
        lambda parts: neighbour_part(*parts, score_scale),
        (query_tiles, keys_nbr, values_nbr, key_valid, local_sum_tiles),
    )
    denominator_local = (
        denominator.reshape(tile_count, HEADS, tile_rows, future_len)
        .transpose(0, 2, 1, 3)
        .reshape(agent_count, HEADS, future_len)
    )
    local_probs = (local_weights / denominator_local[..., None]).astype(jnp.bfloat16)
    mixed_local = jnp.einsum(
        "anck,aknd->acnd", local_probs, values_local, preferred_element_type=jnp.float32
    )
    mixed = (
        (mixed_local.reshape(-1, HEADS, head_size) + mixed_nbr.reshape(-1, HEADS, head_size))
        .astype(jnp.bfloat16)
        .reshape(-1, model_width)
    )
    update = jnp.dot(mixed, w_out, preferred_element_type=jnp.float32)
    denoised = (noisy_future.reshape(-1, model_width).astype(jnp.float32) + update).astype(
        jnp.bfloat16
    )
    denoised = denoised.reshape(agent_count, future_len * model_width)
    packed_new = jnp.dot(packer, denoised, preferred_element_type=jnp.float32).astype(jnp.bfloat16)
    moved_new = exchange(packed_new)
    moved_slots = moved_kept[:, kept.shape[1]].astype(jnp.int32)
    placer = jnp.arange(agent_count, dtype=jnp.int32)[:, None] == moved_slots[None, :]
    placer = placer.astype(jnp.bfloat16)
    placed_kept = jnp.dot(
        placer, moved_kept[:, : kept.shape[1]], preferred_element_type=jnp.float32
    ).astype(jnp.bfloat16)
    placed_new = jnp.dot(placer, moved_new, preferred_element_type=jnp.float32).astype(jnp.bfloat16)
    return jnp.concatenate([placed_kept, placed_new], axis=1).reshape(history.shape)


def solution(mesh):
    in_specs = (
        P(("groups", "region"), None, None),
        P(("groups", "region"), None, None),
        P(),
        P(),
        P(),
        P(),
        P(),
        P(("groups", "region"), None),
        P(("groups", "region"), None),
        P(("groups", "region")),
        P(("groups", "region")),
        P(("groups", "region")),
    )
    out_specs = P(("groups", "region"), None, None)
    return jax.shard_map(
        per_device, mesh=mesh, in_specs=in_specs, out_specs=out_specs, check_vma=False
    )
```
